32 devices in a mesh: grp: 2 (over x), pts: 16 (over z, y, core).
Axes of the slice: x: 2, y: 2, z: 4, core: 2. Of those that a mesh axis runs over, the one named last changes fastest.
Arguments:
- support: bfloat16 [4096, 64], P(('grp', 'pts')), parts along dimension 0, may hold values from -9 to 9
- clouds: bfloat16 [8, 4096, 64], P(None, ('grp', 'pts')), parts along dimension 1, may hold values from -6 to 6
- member_weights: float32 [16], P('grp'), parts along dimension 0, may hold values from 1 to 10
Outputs:
- new_support: float32 [4096, 64], P(('grp', 'pts')), parts along dimension 0
The draws below stay inside these ranges and needn't reach their ends.
There are 2 independent parts, one for each index of `grp`. The reference program is written for one: setup_inputs(seed, part) draws one part's arguments, and reference() takes and returns one part's arrays. A program takes and returns all parts, laid end to end along the dimension named above; each array names one. Nothing has to cross between parts.
All inputs are finite; a program needn't handle non-finite values.
Results may differ from the reference program's by a relative error of at most 0.001.
Values may be sent and summed in bfloat16 or wider, within the bound.
A program may use at most 128 MiB of HBM per device.

```python
import math
import jax
import jax.numpy as jnp
from jax import lax

DIM = 64
MEMB = 8
ITERS = 3
N = 2048
M = 2048


def draw_support(key, part):
    base_key = jax.random.fold_in(key, 11)
    level_key = jax.random.fold_in(key, 12)
    sign_key = jax.random.fold_in(key, 13)
    base = jnp.clip(jax.random.normal(base_key, (N, DIM), jnp.float32), -3.5, 3.5)
    level = jax.random.randint(level_key, (N,), 0, 8)
    strength = jnp.where(level == 5, 3.0, jnp.where(level == 6, 4.0, jnp.where(level == 7, 5.0, 0.0)))
    signs = (2 * jax.random.randint(sign_key, (DIM,), 0, 2) - 1).astype(jnp.float32)
    values = base + strength[:, None] * signs[None, :]
    return jnp.clip(values, -9.0, 9.0).astype(jnp.bfloat16)


def draw_clouds(key, part):
    base_key = jax.random.fold_in(key, 21)
    where_key = jax.random.fold_in(key, 22)
    sign_key = jax.random.fold_in(key, 23)
    base = jnp.clip(jax.random.normal(base_key, (MEMB, M, DIM), jnp.float32), -6.0, 6.0)
    far_row = jax.random.randint(where_key, (MEMB,), 0, M)
    far_sign = (2 * jax.random.randint(sign_key, (MEMB,), 0, 2) - 1).astype(jnp.float32)
    row_index = jnp.arange(M, dtype=jnp.int32)
    is_far = row_index[None, :] == far_row[:, None]
    values = jnp.where(is_far[:, :, None], 6.0 * far_sign[:, None, None], base)
    return values.astype(jnp.bfloat16)


def setup_inputs(seed: int = 0, part: int = 0) -> dict:
    keys = jax.random.split(jax.random.key(seed), 4)
    part_splits = jax.random.split(jax.random.fold_in(keys[3], part), 4)
    return {
        "support": draw_support(jax.random.fold_in(jax.random.fold_in(keys[3], part), 71), part),
        "clouds": draw_clouds(jax.random.fold_in(jax.random.fold_in(keys[3], part), 71), part),
        "member_weights": jnp.clip(jnp.exp(jax.random.uniform(part_splits[2], (MEMB,), jnp.float32, math.log(1.0), math.log(10.0))), 1.0, 10.0),
    }


EPS = 0.05


def tile_cost(points, others):
    cross = lax.dot_general(points, others, (((1,), (1,)), ((), ())), preferred_element_type=jnp.float32)
    wide_a = points.astype(jnp.float32)
    wide_b = others.astype(jnp.float32)
    sq_a = jnp.sum(wide_a * wide_a, axis=1)
    sq_b = jnp.sum(wide_b * wide_b, axis=1)
    return (sq_a[:, None] + sq_b[None, :] - 2.0 * cross) / (2.0 * points.shape[1])


def reference(support, clouds, member_weights):
    count_n = support.shape[0]
    count_m = clouds.shape[1]
    log_n = jnp.log(jnp.float32(count_n))
    log_m = jnp.log(jnp.float32(count_m))
    weights = member_weights / jnp.sum(member_weights)

    def one_member(packed):
        cloud, weight = packed
        cost = tile_cost(support, cloud)
        pot_g = jnp.zeros((count_m,), jnp.float32)
        pot_f = jnp.zeros((count_n,), jnp.float32)
        for step in range(ITERS):
            pot_f = -EPS * jax.nn.logsumexp((pot_g[None, :] - cost) / EPS, axis=1) - EPS * log_n
            pot_g = -EPS * jax.nn.logsumexp((pot_f[:, None] - cost) / EPS, axis=0) - EPS * log_m
        plan = jnp.exp((pot_f[:, None] + pot_g[None, :] - cost) / EPS + log_n).astype(jnp.bfloat16)
        return weight * jnp.dot(plan, cloud, preferred_element_type=jnp.float32)

    terms = lax.map(one_member, (clouds, weights))
    return jnp.sum(terms, axis=0)
```

```python
import functools
import math

import jax
import jax.numpy as jnp
from jax import lax
from jax.experimental import pallas as pl
from jax.experimental.pallas import tpu as pltpu
from jax.sharding import PartitionSpec as P

ITERS = 3
EPS = 0.05
LANES = 128
GROUP = 64
EXTRA = 16
VMEM_BYTES = 56492032
F32 = jnp.float32
BF16 = jnp.bfloat16


def split3(x):
    hi = x.astype(BF16).astype(F32)
    mid = (x - hi).astype(BF16).astype(F32)
    return hi, mid, (x - hi - mid).astype(BF16).astype(F32)


def kernel(
    dims, sup_ref, clouds_ref, weights_hbm, out_ref,
    weights_ref, cloud_send, sup_buf, cloud_buf, left, right, mat, top, best, u_ref, part,
    col, stat_send, stat_recv, plan, out_send, out_recv,
    sup_ssem, sup_rsem, cl_ssem, cl_rsem, relay_ssem, relay_rsem,
    stat_ssem, stat_rsem, out_ssem, out_rsem, own_sem,
):
    memb, sib, shard, dim = dims
    devices = memb * sib
    rows = memb * shard
    cols = devices * shard
    chunk = 2048 if cols % 2048 == 0 else cols
    alpha = math.log2(math.e) / (EPS * 2.0 * dim)
    me = lax.axis_index("pts")
    mine = me // sib
    r = lax.rem(me, sib)

    def peer(d):
        return lax.rem(mine + d, memb)

    def at(cloud, place):
        return {"pts": cloud * sib + place}

    barrier = pltpu.get_barrier_semaphore()
    for d in range(1, memb):
        pl.semaphore_signal(barrier, inc=1, device_id=at(peer(d), r))
    for s in range(1, sib):
        pl.semaphore_signal(barrier, inc=1, device_id=at(mine, lax.rem(r + s, sib)))

    own_sup = pltpu.make_async_copy(sup_ref, sup_buf.at[mine], own_sem.at[0])
    own_cloud = pltpu.make_async_copy(clouds_ref.at[mine], cloud_buf.at[me], own_sem.at[1])
    staged = pltpu.make_async_copy(clouds_ref, cloud_send, own_sem.at[2])
    own_weights = pltpu.make_async_copy(weights_hbm, weights_ref, own_sem.at[3])
    staged.start()
    own_weights.start()
    own_sup.start()
    own_cloud.start()
    own_sup.wait()
    own_cloud.wait()
    staged.wait()
    own_weights.wait()
    pl.semaphore_wait(barrier, memb - 1 + sib - 1)

    def cloud_copy(d):
        target = peer(d)
        return pltpu.make_async_remote_copy(
            cloud_send.at[target], cloud_buf.at[me], cl_ssem.at[d], cl_rsem.at[d],
            device_id=at(target, r), device_id_type=pl.DeviceIdType.MESH)

    def sup_copy(d):
        return pltpu.make_async_remote_copy(
            sup_buf.at[mine], sup_buf.at[mine], sup_ssem.at[d], sup_rsem.at[d],
            device_id=at(peer(d), r), device_id_type=pl.DeviceIdType.MESH)

    def relay_copy(d, s):
        owner = lax.rem(mine + memb - d, memb) * sib + r
        return pltpu.make_async_remote_copy(
            cloud_buf.at[owner], cloud_buf.at[owner], relay_ssem.at[d, s], relay_rsem.at[d, s],
            device_id=at(mine, lax.rem(r + s, sib)), device_id_type=pl.DeviceIdType.MESH)

    order = [memb // 2]
    for d in range(1, memb):
        if d not in order:
            order.append(d)
    for s in range(1, sib):
        relay_copy(0, s).start()
    for d in order:
        cloud_copy(d).start()
    for d in order:
        sup_copy(d).start()

    ones3 = jnp.ones((3, shard), F32)
    zeros = jnp.zeros((EXTRA - 6, shard), F32)

    def make_left(c):
        x = sup_buf[c].astype(F32)
        norm = split3(jnp.sum(x * x, axis=0, keepdims=True) * -alpha)
        block = jnp.concatenate([*split3(x * (2.0 * alpha)), ones3, *norm, zeros], axis=0)
        left[pl.ds(pl.multiple_of(c * shard, shard), shard), :] = jnp.transpose(block).astype(BF16)

    def make_right(q):
        x = cloud_buf[q].astype(F32)
        norm = split3(jnp.sum(x * x, axis=0, keepdims=True) * -alpha)
        block = jnp.concatenate([x, x, x, *norm, ones3, zeros], axis=0)
        right[:, pl.ds(pl.multiple_of(q * shard, shard), shard)] = block.astype(BF16)

    wide = 256

    def nth(i):
        half = memb // 2
        return jnp.where(i == 0, 0, jnp.where(i == 1, half, jnp.where(i <= half, i - 1, i)))

    def owner(d):
        return lax.rem(mine + memb - d, memb)

    def block_of(c):
        return pl.ds(pl.multiple_of(c * shard, shard), shard)

    def cost_rows(c):
        x = left[block_of(c), :]
        high = jnp.full((shard, LANES), -3e38, F32)
        for j in range(0, cols, wide):
            t = jnp.dot(x, right[:, j:j + wide], preferred_element_type=F32)
            mat[block_of(c), j:j + wide] = t
            for i in range(0, wide, LANES):
                high = jnp.maximum(high, t[:, i:i + LANES])
        top[block_of(c), :] = jnp.broadcast_to(jnp.max(high, axis=1, keepdims=True), high.shape)

    def raise_best(c):
        a = top[block_of(c), :]
        for j in range(0, cols, LANES):
            t = mat[block_of(c), j:j + LANES] - a
            high = best[:, j:j + LANES]
            for i in range(0, shard, 8):
                high = jnp.maximum(high, t[i:i + 8])
            best[:, j:j + LANES] = high

    best[...] = jnp.full(best.shape, -3e38, F32)
    make_left(mine)
    make_right(me)

    def take_right(i, _):
        d = nth(i)
        cloud_copy(d).wait_recv()
        for s in range(1, sib):
            relay_copy(d, s).start()
        make_right(owner(d) * sib + r)
        return 0

    def take_relay(i, _):
        d = nth(i)
        for s in range(1, sib):
            relay_copy(d, s).wait_recv()
            make_right(owner(d) * sib + lax.rem(r + sib - s, sib))
        return 0

    def take_left(i, _):
        d = nth(i)
        sup_copy(d).wait_recv()
        make_left(owner(d))
        raise_best(owner(nth(i - 1)))
        cost_rows(owner(d))
        return 0

    lax.fori_loop(1, memb, take_right, 0)
    lax.fori_loop(0, memb, take_relay, 0)
    cost_rows(mine)
    lax.fori_loop(1, memb, take_left, 0)
    raise_best(owner(nth(memb - 1)))

    tiles = chunk // LANES
    groups = rows // GROUP

    def tile(g, base, c):
        return (
            pl.ds(pl.multiple_of(g * GROUP, GROUP), GROUP),
            pl.ds(pl.multiple_of(base + c * LANES, LANES), LANES),
        )

    def rows_of(ref, g):
        return ref[pl.ds(pl.multiple_of(g * GROUP, GROUP), GROUP), :]

    def fold(x, op):
        acc = x[0:8]
        for i in range(8, GROUP, 8):
            acc = op(acc, x[i:i + 8])
        return acc

    def lanes(ref, base, c):
        return ref[:, base + c * LANES:base + (c + 1) * LANES]

    high = jnp.max(best[...], axis=0, keepdims=True)
    stat_send[0] = high
    col[0] = jnp.broadcast_to(high, (8, cols))
    col[1] = jnp.broadcast_to(jnp.exp2(high), (8, cols))

    def stat_copy(step, s):
        n = 2 if step == 0 else 1
        lo = 0 if step == 0 else 1 + step
        return pltpu.make_async_remote_copy(
            stat_send.at[pl.ds(lo, n)], stat_recv.at[s, pl.ds(lo, n)],
            stat_ssem.at[step, s], stat_rsem.at[step, s],
            device_id=at(mine, lax.rem(r + s, sib)), device_id_type=pl.DeviceIdType.MESH)

    def times(x, y):
        return x * jnp.concatenate([y] * (GROUP // 8), axis=0)

    for step in range(ITERS):
        for base in range(0, cols, chunk):
            def row_step(g, _, base=base):
                acc = jnp.zeros((GROUP, LANES), F32)
                a = rows_of(top, g)
                for c in range(tiles):
                    k = mat[tile(g, base, c)]
                    if step == 0:
                        b = jnp.concatenate([lanes(col.at[0], base, c)] * (GROUP // 8), axis=0)
                        k = jnp.exp2((k - a) - b)
                        mat[tile(g, base, c)] = k
                    acc = acc + times(k, lanes(col.at[1], base, c))
                if base > 0:
                    acc = acc + rows_of(part, g)
                part[pl.ds(pl.multiple_of(g * GROUP, GROUP), GROUP), :] = acc
                return 0

            lax.fori_loop(0, groups, row_step, 0, unroll=2)
        total = jnp.sum(part[...], axis=1, keepdims=True)
        u_ref[...] = jnp.broadcast_to(1.0 / (total * rows_all(dims)), u_ref.shape)
        for base in range(0, cols, chunk):
            def col_step(g, acc, base=base):
                u = rows_of(u_ref, g)
                return tuple(
                    acc[c] + fold(mat[tile(g, base, c)] * u, jnp.add) for c in range(tiles))

            start = tuple(jnp.zeros((8, LANES), F32) for _ in range(tiles))
            acc = lax.fori_loop(0, groups, col_step, start, unroll=2)
            for c in range(tiles):
                stat_send[1 + step, :, base + c * LANES:base + (c + 1) * LANES] = jnp.sum(
                    acc[c], axis=0, keepdims=True)
        for s in range(1, sib):
            stat_copy(step, s).start()
        for s in range(1, sib):
            stat_copy(step, s).wait_recv()
        high = stat_send[0]
        for s in range(1, sib):
            high = jnp.maximum(high, stat_recv[s, 0])
        local = jnp.exp2(stat_send[0] - high)
        total = local * stat_send[1 + step]
        for s in range(1, sib):
            total = total + jnp.exp2(stat_recv[s, 0] - high) * stat_recv[s, 1 + step]
        v = local / (total * float(cols))
        col[1] = jnp.broadcast_to(v, (8, cols))

    weight_sum = weights_ref[0]
    for k in range(1, memb):
        weight_sum = weight_sum + weights_ref[k]
    weight = weights_ref[mine] / weight_sum

    def out_copy(target):
        return pltpu.make_async_remote_copy(
            out_send.at[target], out_recv.at[mine], out_ssem.at[target], out_rsem.at[mine],
            device_id=at(target, r), device_id_type=pl.DeviceIdType.MESH)

    def out_arrival(source):
        return pltpu.make_async_remote_copy(
            out_send.at[source], out_recv.at[source], out_ssem.at[source], out_rsem.at[source],
            device_id=at(source, r), device_id_type=pl.DeviceIdType.MESH)

    for block in [0, 4, 1, 5, 2, 6, 3, 7]:
        def plan_step(g, _):
            u = rows_of(u_ref, block * (shard // GROUP) + g) * rows_all(dims)
            for base in range(0, cols, chunk):
                for c in range(tiles):
                    p = times(mat[tile(block * (shard // GROUP) + g, base, c)] * u,
                              lanes(col.at[1], base, c))
                    plan[pl.ds(pl.multiple_of(g * GROUP, GROUP), GROUP),
                         base + c * LANES:base + (c + 1) * LANES] = p.astype(BF16)
            return 0

        lax.fori_loop(0, shard // GROUP, plan_step, 0)
        term = lax.dot_general(
            plan[...], right[:dim, :], (((1,), (1,)), ((), ())), preferred_element_type=F32)
        term = jnp.transpose(term * weight)
        out_send[block] = term

        @pl.when(block != mine)
        def _():
            out_copy(block).start()

    total = out_send[mine]
    for d in range(1, memb):
        out_arrival(peer(d)).wait_recv()
        total = total + out_recv[peer(d)]
    out_ref[...] = total

    for d in range(1, memb):
        cloud_copy(d).wait_send()
        sup_copy(d).wait_send()
        out_copy(peer(d)).wait_send()
    for s in range(1, sib):
        for d in range(memb):
            relay_copy(d, s).wait_send()
        for step in range(ITERS):
            stat_copy(step, s).wait_send()


def rows_all(dims):
    memb, sib, shard, _ = dims
    return float(memb * sib * shard)


def per_device(support, clouds, member_weights):
    devices = lax.axis_size("pts")
    memb, shard, dim = clouds.shape
    sib = devices // memb
    rows, cols = memb * shard, devices * shard
    dims = (memb, sib, shard, dim)
    vmem, dma = pltpu.VMEM, pltpu.SemaphoreType.DMA
    out = pl.pallas_call(
        functools.partial(kernel, dims),
        out_shape=jax.ShapeDtypeStruct((dim, shard), F32),
        in_specs=[
            pl.BlockSpec(memory_space=pltpu.HBM),
            pl.BlockSpec(memory_space=pltpu.HBM),
            pl.BlockSpec(memory_space=pltpu.HBM),
        ],
        out_specs=pl.BlockSpec(memory_space=pltpu.VMEM),
        scratch_shapes=[
            pltpu.SMEM((memb,), F32),
            vmem((memb, dim, shard), BF16),
            vmem((memb, dim, shard), BF16),
            vmem((devices, dim, shard), BF16),
            vmem((rows, 3 * dim + EXTRA), BF16),
            vmem((3 * dim + EXTRA, cols), BF16),
            vmem((rows, cols), F32),
            vmem((rows, LANES), F32),
            vmem((8, cols), F32),
            vmem((rows, LANES), F32),
            vmem((rows, LANES), F32),
            vmem((2, 8, cols), F32),
            vmem((1 + ITERS, 1, cols), F32),
            vmem((sib, 1 + ITERS, 1, cols), F32),
            vmem((shard, cols), BF16),
            vmem((memb, dim, shard), F32),
            vmem((memb, dim, shard), F32),
            dma((memb,)), dma((memb,)),
            dma((memb,)), dma((memb,)),
            dma((memb, sib)), dma((memb, sib)),
            dma((ITERS, sib)), dma((ITERS, sib)),
            dma((memb,)), dma((memb,)), dma((4,)),
        ],
        compiler_params=pltpu.CompilerParams(
            collective_id=0, has_side_effects=True,
            vmem_limit_bytes=VMEM_BYTES),
    )(support.T, clouds.swapaxes(1, 2), member_weights)
    return out.T


def solution(mesh):
    in_specs = (P(("grp", "pts"), None), P(None, ("grp", "pts"), None), P("grp"))
    out_specs = P(("grp", "pts"), None)
    return jax.shard_map(
        per_device, mesh=mesh, in_specs=in_specs, out_specs=out_specs, check_vma=False
    )
```

```python
import functools
import math

import jax
import jax.numpy as jnp
from jax import lax
from jax.experimental import pallas as pl
from jax.experimental.pallas import tpu as pltpu
from jax.sharding import PartitionSpec as P

ITERS = 3
EPS = 0.05
LANES = 128
GROUP = 32
WIDE = 2048
ORDER = (0, 4, 1, 5, 2, 6, 3, 7)
EXTRA = 16
F32 = jnp.float32
BF16 = jnp.bfloat16


def split3(x):
    hi = x.astype(BF16).astype(F32)
    mid = (x - hi).astype(BF16).astype(F32)
    return hi, mid, (x - hi - mid).astype(BF16).astype(F32)


def kernel(
    dims, sup_ref, clouds_ref, weights_hbm, out_ref,
    weights_ref, cloud_send, sup_buf, cloud_buf, left, right, mat, top, best, u_ref, part,
    col, stat_send, stat_recv, plan, out_send, out_recv,
    sup_ssem, sup_rsem, cl_ssem, cl_rsem, relay_ssem, relay_rsem,
    stat_ssem, stat_rsem, out_ssem, out_rsem, own_sem,
):
    memb, sib, shard, dim = dims
    devices = memb * sib
    rows = memb * shard
    cols = devices * shard
    chunk = piece_of(cols)
    alpha = math.log2(math.e) / (EPS * 2.0 * dim)
    me = lax.axis_index("pts")
    mine = me // sib
    r = lax.rem(me, sib)

    def peer(d):
        return jnp.bitwise_xor(mine, d)

    def at(cloud, place):
        return {"pts": cloud * sib + place}

    barrier = pltpu.get_barrier_semaphore()
    for d in range(1, memb):
        pl.semaphore_signal(barrier, inc=1, device_id=at(peer(d), r))
    for s in range(1, sib):
        pl.semaphore_signal(barrier, inc=1, device_id=at(mine, lax.rem(r + s, sib)))

    own_sup = pltpu.make_async_copy(sup_ref, sup_buf.at[mine], own_sem.at[0])
    own_cloud = pltpu.make_async_copy(clouds_ref.at[mine], cloud_buf.at[me], own_sem.at[1])
    staged = pltpu.make_async_copy(clouds_ref, cloud_send, own_sem.at[2])
    own_weights = pltpu.make_async_copy(weights_hbm, weights_ref, own_sem.at[3])
    staged.start()
    own_weights.start()
    own_sup.start()
    own_cloud.start()
    own_sup.wait()
    own_cloud.wait()
    staged.wait()
    own_weights.wait()
    pl.semaphore_wait(barrier, memb - 1 + sib - 1)

    def cloud_copy(d):
        target = peer(d)
        return pltpu.make_async_remote_copy(
            cloud_send.at[target], cloud_buf.at[me], cl_ssem.at[d], cl_rsem.at[d],
            device_id=at(target, r), device_id_type=pl.DeviceIdType.MESH)

    def sup_copy(d):
        return pltpu.make_async_remote_copy(
            sup_buf.at[mine], sup_buf.at[mine], sup_ssem.at[d], sup_rsem.at[d],
            device_id=at(peer(d), r), device_id_type=pl.DeviceIdType.MESH)

    def relay_copy(d, s):
        owner = peer(d) * sib + r
        return pltpu.make_async_remote_copy(
            cloud_buf.at[owner], cloud_buf.at[owner], relay_ssem.at[d, s], relay_rsem.at[d, s],
            device_id=at(mine, lax.rem(r + s, sib)), device_id_type=pl.DeviceIdType.MESH)

    near = list(range(1, memb // 2))
    far = list(reversed(range(memb // 2, memb)))
    for s in range(1, sib):
        relay_copy(0, s).start()
    for d in far + near:
        cloud_copy(d).start()
    for d in near + far:
        sup_copy(d).start()

    ones3 = jnp.ones((3, shard), F32)
    zeros = jnp.zeros((EXTRA - 6, shard), F32)

    def make_left(c):
        x = sup_buf[c].astype(F32)
        norm = split3(jnp.sum(x * x, axis=0, keepdims=True) * -alpha)
        block = jnp.concatenate([*split3(x * (2.0 * alpha)), ones3, *norm, zeros], axis=0)
        left[pl.ds(pl.multiple_of(c * shard, shard), shard), :] = jnp.transpose(block).astype(BF16)

    def make_right(q):
        x = cloud_buf[q].astype(F32)
        norm = split3(jnp.sum(x * x, axis=0, keepdims=True) * -alpha)
        block = jnp.concatenate([x, x, x, *norm, ones3, zeros], axis=0)
        right[:, pl.ds(pl.multiple_of(q * shard, shard), shard)] = block.astype(BF16)

    wide = 256

    def block_of(c):
        return pl.ds(pl.multiple_of(c * shard, shard), shard)

    def sweep(body, start):
        if cols <= WIDE:
            return body(0, start)
        return lax.fori_loop(
            0, cols // WIDE, lambda n, t: body(pl.multiple_of(n * WIDE, WIDE), t), start)

    def cost_rows(c):
        x = left[block_of(c), :]

        def step(base, high):
            for j in range(0, min(cols, WIDE), wide):
                t = jnp.dot(x, right[:, pl.ds(base + j, wide)], preferred_element_type=F32)
                mat[block_of(c), pl.ds(base + j, wide)] = t
                for i in range(0, wide, LANES):
                    high = jnp.maximum(high, t[:, i:i + LANES])
            return high

        high = sweep(step, jnp.full((shard, LANES), -3e38, F32))
        top[block_of(c), :] = jnp.broadcast_to(jnp.max(high, axis=1, keepdims=True), high.shape)

    def raise_best(c):
        a = top[block_of(c), :]

        def step(base, _):
            for j in range(0, min(cols, WIDE), LANES):
                span = pl.ds(base + j, LANES)
                t = mat[block_of(c), span] - a
                high = best[:, span]
                for i in range(0, shard, 8):
                    high = jnp.maximum(high, t[i:i + 8])
                best[:, span] = high
            return 0

        sweep(step, 0)

    best[...] = jnp.full(best.shape, -3e38, F32)
    make_left(mine)
    make_right(me)

    def take_right(i, _):
        make_right(peer(i) * sib + r)
        return 0

    def take_relay(i, _):
        for s in range(1, sib):
            make_right(peer(i) * sib + lax.rem(r + sib - s, sib))
        return 0

    for d in near + far:
        cloud_copy(d).wait_recv()
        for s in range(1, sib):
            relay_copy(d, s).start()
    lax.fori_loop(1, memb, take_right, 0, unroll=7)
    for d in range(memb):
        for s in range(1, sib):
            relay_copy(d, s).wait_recv()
    lax.fori_loop(0, memb, take_relay, 0, unroll=4)
    def take_rows(turn):
        for d in turn:
            if d > 0:
                sup_copy(d).wait_recv()
        for d in turn:
            if d > 0:
                make_left(peer(d))
        for n, d in enumerate(turn):
            cost_rows(peer(d))
            if n > 0:
                raise_best(peer(turn[n - 1]))
        raise_best(peer(turn[-1]))

    take_rows([0] + near)
    take_rows(far)

    tiles = chunk // LANES
    groups = rows // GROUP
    unroll = groups if cols <= WIDE else 2

    def tile(g, base, c):
        return (
            pl.ds(pl.multiple_of(g * GROUP, GROUP), GROUP),
            pl.ds(pl.multiple_of(base + c * LANES, LANES), LANES),
        )

    def rows_of(ref, g):
        return ref[pl.ds(pl.multiple_of(g * GROUP, GROUP), GROUP), :]

    def fold(x, op):
        acc = x[0:8]
        for i in range(8, GROUP, 8):
            acc = op(acc, x[i:i + 8])
        return acc

    def lanes(ref, base, c):
        return ref[:, base + c * LANES:base + (c + 1) * LANES]

    high = jnp.max(best[...], axis=0, keepdims=True)
    stat_send[0] = high
    col[0] = jnp.broadcast_to(high, (8, cols))
    col[1] = jnp.broadcast_to(jnp.exp2(high), (8, cols))

    pieces = cols // chunk

    def high_copy(s):
        return pltpu.make_async_remote_copy(
            stat_send.at[0], stat_recv.at[s, 0],
            stat_ssem.at[0, s], stat_rsem.at[0, s],
            device_id=at(mine, lax.rem(r + s, sib)), device_id_type=pl.DeviceIdType.MESH)

    def stat_copy(step, n, s):
        span = pl.ds(n * chunk, chunk)
        place = 1 + step * pieces + n
        return pltpu.make_async_remote_copy(
            stat_send.at[1 + step, :, span], stat_recv.at[s, 1 + step, :, span],
            stat_ssem.at[place, s], stat_rsem.at[place, s],
            device_id=at(mine, lax.rem(r + s, sib)), device_id_type=pl.DeviceIdType.MESH)

    def take_stat(step, n):
        span = slice(n * chunk, n * chunk + chunk)
        for s in range(1, sib):
            if step == 0 and n == 0:
                high_copy(s).wait_recv()
            stat_copy(step, n, s).wait_recv()
        high = stat_send[0, :, span]
        for s in range(1, sib):
            high = jnp.maximum(high, stat_recv[s, 0, :, span])
        local = jnp.exp2(stat_send[0, :, span] - high)
        total = local * stat_send[1 + step, :, span]
        for s in range(1, sib):
            total = total + jnp.exp2(stat_recv[s, 0, :, span] - high) * stat_recv[s, 1 + step, :, span]
        col[1, :, span] = jnp.broadcast_to(local / (total * float(cols)), (8, chunk))

    for s in range(1, sib):
        high_copy(s).start()

    def times(x, y):
        return x * jnp.concatenate([y] * (GROUP // 8), axis=0)

    for step in range(ITERS):
        for base in range(0, cols, chunk):
            if step > 0:
                take_stat(step - 1, base // chunk)

            def row_step(g, _, base=base):
                acc = jnp.zeros((GROUP, LANES), F32)
                a = rows_of(top, g)
                for c in range(tiles):
                    k = mat[tile(g, base, c)]
                    if step == 0:
                        b = jnp.concatenate([lanes(col.at[0], base, c)] * (GROUP // 8), axis=0)
                        k = jnp.exp2((k - a) - b)
                        mat[tile(g, base, c)] = k
                    acc = acc + times(k, lanes(col.at[1], base, c))
                if base > 0:
                    acc = acc + rows_of(part, g)
                span = pl.ds(pl.multiple_of(g * GROUP, GROUP), GROUP)
                if base + chunk < cols:
                    part[span, :] = acc
                else:
                    total = jnp.sum(acc, axis=1, keepdims=True)
                    u_ref[span, :] = jnp.broadcast_to(1.0 / (total * rows_all(dims)), acc.shape)
                return 0

            lax.fori_loop(0, groups, row_step, 0, unroll=unroll)
        for base in range(0, cols, chunk):
            def col_step(g, acc, base=base):
                u = rows_of(u_ref, g)
                return tuple(
                    acc[c] + fold(mat[tile(g, base, c)] * u, jnp.add) for c in range(tiles))

            start = tuple(jnp.zeros((8, LANES), F32) for _ in range(tiles))
            acc = lax.fori_loop(0, groups, col_step, start, unroll=unroll)
            for c in range(tiles):
                stat_send[1 + step, :, base + c * LANES:base + (c + 1) * LANES] = jnp.sum(
                    acc[c], axis=0, keepdims=True)
            for s in range(1, sib):
                stat_copy(step, base // chunk, s).start()

    for n in range(pieces):
        take_stat(ITERS - 1, n)

    weight_sum = weights_ref[0]
    for k in range(1, memb):
        weight_sum = weight_sum + weights_ref[k]
    weight = weights_ref[mine] / weight_sum

    def out_copy(target):
        return pltpu.make_async_remote_copy(
            out_send.at[target], out_recv.at[mine], out_ssem.at[target], out_rsem.at[mine],
            device_id=at(target, r), device_id_type=pl.DeviceIdType.MESH)

    def out_arrival(source):
        return pltpu.make_async_remote_copy(
            out_send.at[source], out_recv.at[source], out_ssem.at[source], out_rsem.at[source],
            device_id=at(source, r), device_id_type=pl.DeviceIdType.MESH)

    for n, block in enumerate(ORDER):
        u = u_ref[block * shard:(block + 1) * shard, :] * rows_all(dims)

        def plan_step(base, _):
            for j in range(0, min(cols, WIDE), LANES):
                span = pl.ds(base + j, LANES)
                p = mat[block * shard:(block + 1) * shard, span] * u
                v = jnp.concatenate([col[1, :, span]] * (shard // 8), axis=0)
                plan[n % 2, :, span] = (p * v).astype(BF16)
            return 0

        sweep(plan_step, 0)
        term = lax.dot_general(
            right[:dim, :], plan[n % 2], (((1,), (1,)), ((), ())), preferred_element_type=F32)
        out_send[block] = term * weight

        @pl.when(block != mine)
        def _():
            out_copy(block).start()

    total = out_send[mine]
    for d in range(1, memb):
        out_arrival(peer(d)).wait_recv()
        total = total + out_recv[peer(d)]
    out_ref[...] = total

    for d in range(1, memb):
        cloud_copy(d).wait_send()
        sup_copy(d).wait_send()
        out_copy(peer(d)).wait_send()
    for s in range(1, sib):
        for d in range(memb):
            relay_copy(d, s).wait_send()
        high_copy(s).wait_send()
        for step in range(ITERS):
            for n in range(pieces):
                stat_copy(step, n, s).wait_send()


def piece_of(cols):
    return cols // 2 if cols <= WIDE else WIDE


def rows_all(dims):
    memb, sib, shard, _ = dims
    return float(memb * sib * shard)


def per_device(support, clouds, member_weights):
    devices = lax.axis_size("pts")
    memb, shard, dim = clouds.shape
    sib = devices // memb
    rows, cols = memb * shard, devices * shard
    dims = (memb, sib, shard, dim)
    pieces = cols // piece_of(cols)
    vmem, dma = pltpu.VMEM, pltpu.SemaphoreType.DMA
    out = pl.pallas_call(
        functools.partial(kernel, dims),
        out_shape=jax.ShapeDtypeStruct((dim, shard), F32),
        in_specs=[
            pl.BlockSpec(memory_space=pltpu.HBM),
            pl.BlockSpec(memory_space=pltpu.HBM),
            pl.BlockSpec(memory_space=pltpu.HBM),
        ],
        out_specs=pl.BlockSpec(memory_space=pltpu.VMEM),
        scratch_shapes=[
            pltpu.SMEM((memb,), F32),
            vmem((memb, dim, shard), BF16),
            vmem((memb, dim, shard), BF16),
            vmem((devices, dim, shard), BF16),
            vmem((rows, 3 * dim + EXTRA), BF16),
            vmem((3 * dim + EXTRA, cols), BF16),
            vmem((rows, cols), F32),
            vmem((rows, LANES), F32),
            vmem((8, cols), F32),
            vmem((rows, LANES), F32),
            vmem((rows, LANES), F32),
            vmem((2, 8, cols), F32),
            vmem((1 + ITERS, 1, cols), F32),
            vmem((sib, 1 + ITERS, 1, cols), F32),
            vmem((2, shard, cols), BF16),
            vmem((memb, dim, shard), F32),
            vmem((memb, dim, shard), F32),
            dma((memb,)), dma((memb,)),
            dma((memb,)), dma((memb,)),
            dma((memb, sib)), dma((memb, sib)),
            dma((1 + ITERS * pieces, sib)), dma((1 + ITERS * pieces, sib)),
            dma((memb,)), dma((memb,)), dma((4,)),
        ],
        compiler_params=pltpu.CompilerParams(
            collective_id=0, has_side_effects=True,
            vmem_limit_bytes=rows * cols * 4 + (24 << 20)),
    )(*(pltpu.with_memory_space_constraint(x, pltpu.HBM)
        for x in (support.T, clouds.swapaxes(1, 2), member_weights)))
    return out.T


def solution(mesh):
    in_specs = (P(("grp", "pts"), None), P(None, ("grp", "pts"), None), P("grp"))
    out_specs = P(("grp", "pts"), None)
    return jax.shard_map(
        per_device, mesh=mesh, in_specs=in_specs, out_specs=out_specs, check_vma=False
    )
```

```python
import functools
import math

import jax
import jax.numpy as jnp
from jax import lax
from jax.experimental import pallas as pl
from jax.experimental.pallas import tpu as pltpu
from jax.sharding import PartitionSpec as P

ITERS = 3
EPS = 0.05
LANES = 128
GROUP = 32
WIDE = 2048
ORDER = (0, 4, 1, 5, 2, 6, 3, 7)
EXTRA = 16
F32 = jnp.float32
BF16 = jnp.bfloat16


def split3(x):
    hi = x.astype(BF16).astype(F32)
    mid = (x - hi).astype(BF16).astype(F32)
    return hi, mid, (x - hi - mid).astype(BF16).astype(F32)


def kernel(
    dims, sup_ref, clouds_ref, weights_hbm, out_ref,
    weights_ref, cloud_send, sup_buf, cloud_buf, left, right, mat, top, best, u_ref, part,
    col, share, stat_send, stat_recv, plan, out_send, out_recv,
    sup_ssem, sup_rsem, cl_ssem, cl_rsem, relay_ssem, relay_rsem,
    stat_ssem, stat_rsem, out_ssem, out_rsem, own_sem,
):
    memb, sib, shard, dim = dims
    devices = memb * sib
    rows = memb * shard
    cols = devices * shard
    chunk = piece_of(cols)
    alpha = math.log2(math.e) / (EPS * 2.0 * dim)
    me = lax.axis_index("pts")
    mine = me // sib
    r = lax.rem(me, sib)

    def peer(d):
        return jnp.bitwise_xor(mine, d)

    def at(cloud, place):
        return {"pts": cloud * sib + place}

    barrier = pltpu.get_barrier_semaphore()
    for d in range(1, memb):
        pl.semaphore_signal(barrier, inc=1, device_id=at(peer(d), r))
    for s in range(1, sib):
        pl.semaphore_signal(barrier, inc=1, device_id=at(mine, lax.rem(r + s, sib)))

    own_sup = pltpu.make_async_copy(sup_ref, sup_buf.at[mine], own_sem.at[0])
    own_cloud = pltpu.make_async_copy(clouds_ref.at[mine], cloud_buf.at[me], own_sem.at[1])
    staged = pltpu.make_async_copy(clouds_ref, cloud_send, own_sem.at[2])
    own_weights = pltpu.make_async_copy(weights_hbm, weights_ref, own_sem.at[3])
    staged.start()
    own_weights.start()
    own_sup.start()
    own_cloud.start()
    own_sup.wait()
    own_cloud.wait()
    staged.wait()
    own_weights.wait()
    pl.semaphore_wait(barrier, memb - 1 + sib - 1)

    def cloud_copy(d):
        target = peer(d)
        return pltpu.make_async_remote_copy(
            cloud_send.at[target], cloud_buf.at[me], cl_ssem.at[d], cl_rsem.at[d],
            device_id=at(target, r), device_id_type=pl.DeviceIdType.MESH)

    def sup_copy(d):
        return pltpu.make_async_remote_copy(
            sup_buf.at[mine], sup_buf.at[mine], sup_ssem.at[d], sup_rsem.at[d],
            device_id=at(peer(d), r), device_id_type=pl.DeviceIdType.MESH)

    def relay_copy(d, s):
        owner = peer(d) * sib + r
        return pltpu.make_async_remote_copy(
            cloud_buf.at[owner], cloud_buf.at[owner], relay_ssem.at[d, s], relay_rsem.at[d, s],
            device_id=at(mine, lax.rem(r + s, sib)), device_id_type=pl.DeviceIdType.MESH)

    near = list(range(1, memb // 2))
    far = list(reversed(range(memb // 2, memb)))
    for s in range(1, sib):
        relay_copy(0, s).start()
    for d in far + near:
        cloud_copy(d).start()
    for d in near + far:
        sup_copy(d).start()

    ones3 = jnp.ones((3, shard), F32)
    zeros = jnp.zeros((EXTRA - 6, shard), F32)

    def make_left(c):
        x = sup_buf[c].astype(F32)
        norm = split3(jnp.sum(x * x, axis=0, keepdims=True) * -alpha)
        block = jnp.concatenate([*split3(x * (2.0 * alpha)), ones3, *norm, zeros], axis=0)
        left[pl.ds(pl.multiple_of(c * shard, shard), shard), :] = jnp.transpose(block).astype(BF16)

    def make_right(q):
        x = cloud_buf[q].astype(F32)
        norm = split3(jnp.sum(x * x, axis=0, keepdims=True) * -alpha)
        block = jnp.concatenate([x, x, x, *norm, ones3, zeros], axis=0)
        right[:, pl.ds(pl.multiple_of(q * shard, shard), shard)] = block.astype(BF16)

    wide = 256

    def block_of(c):
        return pl.ds(pl.multiple_of(c * shard, shard), shard)

    def sweep(body, start):
        if cols <= WIDE:
            return body(0, start)
        return lax.fori_loop(
            0, cols // WIDE, lambda n, t: body(pl.multiple_of(n * WIDE, WIDE), t), start)

    def cost_rows(c):
        x = left[block_of(c), :]

        def step(base, high):
            for j in range(0, min(cols, WIDE), wide):
                t = jnp.dot(x, right[:, pl.ds(base + j, wide)], preferred_element_type=F32)
                mat[block_of(c), pl.ds(base + j, wide)] = t
                for i in range(0, wide, LANES):
                    high = jnp.maximum(high, t[:, i:i + LANES])
            return high

        high = sweep(step, jnp.full((shard, LANES), -3e38, F32))
        top[block_of(c), :] = jnp.broadcast_to(jnp.max(high, axis=1, keepdims=True), high.shape)

    def raise_best(c):
        a = top[block_of(c), :]

        def step(base, _):
            for j in range(0, min(cols, WIDE), LANES):
                span = pl.ds(base + j, LANES)
                t = mat[block_of(c), span] - a
                high = best[:, span]
                for i in range(0, shard, 8):
                    high = jnp.maximum(high, t[i:i + 8])
                best[:, span] = high
            return 0

        sweep(step, 0)

    best[...] = jnp.full(best.shape, -3e38, F32)
    make_left(mine)
    make_right(me)

    def take_right(i, _):
        make_right(peer(i) * sib + r)
        return 0

    def take_relay(i, _):
        for s in range(1, sib):
            make_right(peer(i) * sib + lax.rem(r + sib - s, sib))
        return 0

    for d in near + far:
        cloud_copy(d).wait_recv()
        for s in range(1, sib):
            relay_copy(d, s).start()
    lax.fori_loop(1, memb, take_right, 0, unroll=7)
    for d in range(memb):
        for s in range(1, sib):
            relay_copy(d, s).wait_recv()
    lax.fori_loop(0, memb, take_relay, 0, unroll=4)
    def take_rows(turn):
        for d in turn:
            if d > 0:
                sup_copy(d).wait_recv()
        for d in turn:
            if d > 0:
                make_left(peer(d))
        for n, d in enumerate(turn):
            cost_rows(peer(d))
            if n > 0:
                raise_best(peer(turn[n - 1]))
        raise_best(peer(turn[-1]))

    take_rows([0] + near)
    take_rows(far)

    tiles = chunk // LANES
    groups = rows // GROUP
    unroll = groups if cols <= WIDE else 2

    def tile(g, base, c):
        return (
            pl.ds(pl.multiple_of(g * GROUP, GROUP), GROUP),
            pl.ds(pl.multiple_of(base + c * LANES, LANES), LANES),
        )

    def rows_of(ref, g):
        return ref[pl.ds(pl.multiple_of(g * GROUP, GROUP), GROUP), :]

    def fold(x, op):
        acc = x[0:8]
        for i in range(8, GROUP, 8):
            acc = op(acc, x[i:i + 8])
        return acc

    def lanes(ref, base, c):
        return ref[:, base + c * LANES:base + (c + 1) * LANES]

    high = jnp.max(best[...], axis=0, keepdims=True)
    stat_send[0] = high
    col[0] = jnp.broadcast_to(high, (8, cols))
    col[1] = jnp.broadcast_to(jnp.exp2(high), (8, cols))

    pieces = cols // chunk

    def high_copy(s):
        return pltpu.make_async_remote_copy(
            stat_send.at[0], stat_recv.at[s, 0],
            stat_ssem.at[0, s], stat_rsem.at[0, s],
            device_id=at(mine, lax.rem(r + s, sib)), device_id_type=pl.DeviceIdType.MESH)

    def stat_copy(step, n, s):
        span = pl.ds(n * chunk, chunk)
        place = 1 + step * pieces + n
        return pltpu.make_async_remote_copy(
            stat_send.at[1 + step, :, span], stat_recv.at[s, 1 + step, :, span],
            stat_ssem.at[place, s], stat_rsem.at[place, s],
            device_id=at(mine, lax.rem(r + s, sib)), device_id_type=pl.DeviceIdType.MESH)

    def take_stat(step, n):
        span = slice(n * chunk, n * chunk + chunk)
        for s in range(1, sib):
            if step == 0 and n == 0:
                high_copy(s).wait_recv()
            stat_copy(step, n, s).wait_recv()
        if step == 0:
            high = stat_send[0, :, span]
            for s in range(1, sib):
                high = jnp.maximum(high, stat_recv[s, 0, :, span])
            share[0, :, span] = jnp.exp2(stat_send[0, :, span] - high)
            for s in range(1, sib):
                share[s, :, span] = jnp.exp2(stat_recv[s, 0, :, span] - high)
        local = share[0, :, span]
        total = local * stat_send[1 + step, :, span]
        for s in range(1, sib):
            total = total + share[s, :, span] * stat_recv[s, 1 + step, :, span]
        col[1, :, span] = jnp.broadcast_to(local / (total * float(cols)), (8, chunk))

    for s in range(1, sib):
        high_copy(s).start()

    def times(x, y):
        return x * jnp.concatenate([y] * (GROUP // 8), axis=0)

    for step in range(ITERS):
        for base in range(0, cols, chunk):
            if step > 0:
                take_stat(step - 1, base // chunk)

            def row_step(g, _, base=base):
                acc = jnp.zeros((GROUP, LANES), F32)
                a = rows_of(top, g)
                for c in range(tiles):
                    k = mat[tile(g, base, c)]
                    if step == 0:
                        b = jnp.concatenate([lanes(col.at[0], base, c)] * (GROUP // 8), axis=0)
                        k = jnp.exp2((k - a) - b)
                        mat[tile(g, base, c)] = k
                    acc = acc + times(k, lanes(col.at[1], base, c))
                if base > 0:
                    acc = acc + rows_of(part, g)
                span = pl.ds(pl.multiple_of(g * GROUP, GROUP), GROUP)
                if base + chunk < cols:
                    part[span, :] = acc
                else:
                    total = jnp.sum(acc, axis=1, keepdims=True)
                    u_ref[span, :] = jnp.broadcast_to(1.0 / (total * rows_all(dims)), acc.shape)
                return 0

            lax.fori_loop(0, groups, row_step, 0, unroll=unroll)
        for base in range(0, cols, chunk):
            def col_step(g, acc, base=base):
                u = rows_of(u_ref, g)
                return tuple(
                    acc[c] + fold(mat[tile(g, base, c)] * u, jnp.add) for c in range(tiles))

            start = tuple(jnp.zeros((8, LANES), F32) for _ in range(tiles))
            acc = lax.fori_loop(0, groups, col_step, start, unroll=unroll)
            for c in range(tiles):
                stat_send[1 + step, :, base + c * LANES:base + (c + 1) * LANES] = jnp.sum(
                    acc[c], axis=0, keepdims=True)
            for s in range(1, sib):
                stat_copy(step, base // chunk, s).start()

    for n in range(pieces):
        take_stat(ITERS - 1, n)

    weight_sum = weights_ref[0]
    for k in range(1, memb):
        weight_sum = weight_sum + weights_ref[k]
    weight = weights_ref[mine] / weight_sum

    def out_copy(target):
        return pltpu.make_async_remote_copy(
            out_send.at[target], out_recv.at[mine], out_ssem.at[target], out_rsem.at[mine],
            device_id=at(target, r), device_id_type=pl.DeviceIdType.MESH)

    def out_arrival(source):
        return pltpu.make_async_remote_copy(
            out_send.at[source], out_recv.at[source], out_ssem.at[source], out_rsem.at[source],
            device_id=at(source, r), device_id_type=pl.DeviceIdType.MESH)

    for n, block in enumerate(ORDER):
        u = u_ref[block * shard:(block + 1) * shard, :] * rows_all(dims)

        def plan_step(base, _):
            for j in range(0, min(cols, WIDE), LANES):
                span = pl.ds(base + j, LANES)
                p = mat[block * shard:(block + 1) * shard, span] * u
                v = jnp.concatenate([col[1, :, span]] * (shard // 8), axis=0)
                plan[n % 2, :, span] = (p * v).astype(BF16)
            return 0

        sweep(plan_step, 0)
        term = lax.dot_general(
            right[:dim, :], plan[n % 2], (((1,), (1,)), ((), ())), preferred_element_type=F32)
        out_send[block] = term * weight

        @pl.when(block != mine)
        def _():
            out_copy(block).start()

    total = out_send[mine]
    for d in range(1, memb):
        out_arrival(peer(d)).wait_recv()
        total = total + out_recv[peer(d)]
    out_ref[...] = total

    for d in range(1, memb):
        cloud_copy(d).wait_send()
        sup_copy(d).wait_send()
        out_copy(peer(d)).wait_send()
    for s in range(1, sib):
        for d in range(memb):
            relay_copy(d, s).wait_send()
        high_copy(s).wait_send()
        for step in range(ITERS):
            for n in range(pieces):
                stat_copy(step, n, s).wait_send()


def piece_of(cols):
    return cols // 2 if cols <= WIDE else WIDE


def rows_all(dims):
    memb, sib, shard, _ = dims
    return float(memb * sib * shard)


def per_device(support, clouds, member_weights):
    devices = lax.axis_size("pts")
    memb, shard, dim = clouds.shape
    sib = devices // memb
    rows, cols = memb * shard, devices * shard
    dims = (memb, sib, shard, dim)
    pieces = cols // piece_of(cols)
    vmem, dma = pltpu.VMEM, pltpu.SemaphoreType.DMA
    out = pl.pallas_call(
        functools.partial(kernel, dims),
        out_shape=jax.ShapeDtypeStruct((dim, shard), F32),
        in_specs=[
            pl.BlockSpec(memory_space=pltpu.HBM),
            pl.BlockSpec(memory_space=pltpu.HBM),
            pl.BlockSpec(memory_space=pltpu.HBM),
        ],
        out_specs=pl.BlockSpec(memory_space=pltpu.VMEM),
        scratch_shapes=[
            pltpu.SMEM((memb,), F32),
            vmem((memb, dim, shard), BF16),
            vmem((memb, dim, shard), BF16),
            vmem((devices, dim, shard), BF16),
            vmem((rows, 3 * dim + EXTRA), BF16),
            vmem((3 * dim + EXTRA, cols), BF16),
            vmem((rows, cols), F32),
            vmem((rows, LANES), F32),
            vmem((8, cols), F32),
            vmem((rows, LANES), F32),
            vmem((rows, LANES), F32),
            vmem((2, 8, cols), F32),
            vmem((sib, 1, cols), F32),
            vmem((1 + ITERS, 1, cols), F32),
            vmem((sib, 1 + ITERS, 1, cols), F32),
            vmem((2, shard, cols), BF16),
            vmem((memb, dim, shard), F32),
            vmem((memb, dim, shard), F32),
            dma((memb,)), dma((memb,)),
            dma((memb,)), dma((memb,)),
            dma((memb, sib)), dma((memb, sib)),
            dma((1 + ITERS * pieces, sib)), dma((1 + ITERS * pieces, sib)),
            dma((memb,)), dma((memb,)), dma((4,)),
        ],
        compiler_params=pltpu.CompilerParams(
            collective_id=0, has_side_effects=True,
            vmem_limit_bytes=rows * cols * 4 + (24 << 20)),
    )(*(pltpu.with_memory_space_constraint(x, pltpu.HBM)
        for x in (support.T, clouds.swapaxes(1, 2), member_weights)))
    return out.T


def solution(mesh):
    in_specs = (P(("grp", "pts"), None), P(None, ("grp", "pts"), None), P("grp"))
    out_specs = P(("grp", "pts"), None)
    return jax.shard_map(
        per_device, mesh=mesh, in_specs=in_specs, out_specs=out_specs, check_vma=False
    )
```

```python
import functools
import math

import jax
import jax.numpy as jnp
from jax import lax
from jax.experimental import pallas as pl
from jax.experimental.pallas import tpu as pltpu
from jax.sharding import PartitionSpec as P

ITERS = 3
EPS = 0.05
LANES = 128
GROUP = 32
WIDE = 2048
ORDER = (0, 4, 1, 5, 2, 6, 3, 7)
TURNS = (ORDER[:1], ORDER[1:3], ORDER[3:5], ORDER[5:])
EXTRA = 16
F32 = jnp.float32
BF16 = jnp.bfloat16


def split3(x):
    hi = x.astype(BF16).astype(F32)
    mid = (x - hi).astype(BF16).astype(F32)
    return hi, mid, (x - hi - mid).astype(BF16).astype(F32)


def kernel(
    dims, sup_ref, clouds_ref, weights_hbm, out_ref,
    weights_ref, cloud_send, sup_buf, cloud_buf, left, right, mat, top, best, u_ref, part,
    col, share, stat_send, stat_recv, plan, out_send, out_recv,
    sup_ssem, sup_rsem, cl_ssem, cl_rsem, relay_ssem, relay_rsem,
    stat_ssem, stat_rsem, out_ssem, out_rsem, own_sem,
):
    memb, sib, shard, dim = dims
    devices = memb * sib
    rows = memb * shard
    cols = devices * shard
    chunk = piece_of(cols)
    alpha = math.log2(math.e) / (EPS * 2.0 * dim)
    me = lax.axis_index("pts")
    mine = me // sib
    r = lax.rem(me, sib)

    def peer(d):
        return jnp.bitwise_xor(mine, d)

    def at(cloud, place):
        return {"pts": cloud * sib + place}

    barrier = pltpu.get_barrier_semaphore()
    for d in range(1, memb):
        pl.semaphore_signal(barrier, inc=1, device_id=at(peer(d), r))
    for s in range(1, sib):
        pl.semaphore_signal(barrier, inc=1, device_id=at(mine, lax.rem(r + s, sib)))

    own_sup = pltpu.make_async_copy(sup_ref, sup_buf.at[mine], own_sem.at[0])
    own_cloud = pltpu.make_async_copy(clouds_ref.at[mine], cloud_buf.at[me], own_sem.at[1])
    staged = pltpu.make_async_copy(clouds_ref, cloud_send, own_sem.at[2])
    own_weights = pltpu.make_async_copy(weights_hbm, weights_ref, own_sem.at[3])
    staged.start()
    own_weights.start()
    own_sup.start()
    own_cloud.start()
    own_sup.wait()
    own_cloud.wait()
    staged.wait()
    own_weights.wait()
    pl.semaphore_wait(barrier, memb - 1 + sib - 1)

    def cloud_copy(d):
        target = peer(d)
        return pltpu.make_async_remote_copy(
            cloud_send.at[target], cloud_buf.at[me], cl_ssem.at[d], cl_rsem.at[d],
            device_id=at(target, r), device_id_type=pl.DeviceIdType.MESH)

    def sup_copy(d):
        return pltpu.make_async_remote_copy(
            sup_buf.at[mine], sup_buf.at[mine], sup_ssem.at[d], sup_rsem.at[d],
            device_id=at(peer(d), r), device_id_type=pl.DeviceIdType.MESH)

    def relay_copy(d, s):
        owner = peer(d) * sib + r
        return pltpu.make_async_remote_copy(
            cloud_buf.at[owner], cloud_buf.at[owner], relay_ssem.at[d, s], relay_rsem.at[d, s],
            device_id=at(mine, lax.rem(r + s, sib)), device_id_type=pl.DeviceIdType.MESH)

    near = list(range(1, memb // 2))
    far = list(reversed(range(memb // 2, memb)))
    for s in range(1, sib):
        relay_copy(0, s).start()
    for d in far + near:
        cloud_copy(d).start()
    for d in near + far:
        sup_copy(d).start()

    ones3 = jnp.ones((3, shard), F32)
    zeros = jnp.zeros((EXTRA - 6, shard), F32)

    def make_left(c):
        x = sup_buf[c].astype(F32)
        norm = split3(jnp.sum(x * x, axis=0, keepdims=True) * -alpha)
        block = jnp.concatenate([*split3(x * (2.0 * alpha)), ones3, *norm, zeros], axis=0)
        left[pl.ds(pl.multiple_of(c * shard, shard), shard), :] = jnp.transpose(block).astype(BF16)

    def make_right(q):
        x = cloud_buf[q].astype(F32)
        norm = split3(jnp.sum(x * x, axis=0, keepdims=True) * -alpha)
        block = jnp.concatenate([x, x, x, *norm, ones3, zeros], axis=0)
        right[:, pl.ds(pl.multiple_of(q * shard, shard), shard)] = block.astype(BF16)

    wide = 256

    def block_of(c):
        return pl.ds(pl.multiple_of(c * shard, shard), shard)

    def sweep(body, start):
        if cols <= WIDE:
            return body(0, start)
        return lax.fori_loop(
            0, cols // WIDE, lambda n, t: body(pl.multiple_of(n * WIDE, WIDE), t), start)

    def cost_rows(c):
        x = left[block_of(c), :]

        def step(base, high):
            for j in range(0, min(cols, WIDE), wide):
                t = jnp.dot(x, right[:, pl.ds(base + j, wide)], preferred_element_type=F32)
                mat[block_of(c), pl.ds(base + j, wide)] = t
                for i in range(0, wide, LANES):
                    high = jnp.maximum(high, t[:, i:i + LANES])
            return high

        high = sweep(step, jnp.full((shard, LANES), -3e38, F32))
        top[block_of(c), :] = jnp.broadcast_to(jnp.max(high, axis=1, keepdims=True), high.shape)

    def raise_best(c):
        a = top[block_of(c), :]

        def step(base, _):
            for j in range(0, min(cols, WIDE), LANES):
                span = pl.ds(base + j, LANES)
                t = mat[block_of(c), span] - a
                high = best[:, span]
                for i in range(0, shard, 8):
                    high = jnp.maximum(high, t[i:i + 8])
                best[:, span] = high
            return 0

        sweep(step, 0)

    best[...] = jnp.full(best.shape, -3e38, F32)
    make_left(mine)
    make_right(me)

    def take_right(i, _):
        make_right(peer(i) * sib + r)
        return 0

    def take_relay(i, _):
        for s in range(1, sib):
            make_right(peer(i) * sib + lax.rem(r + sib - s, sib))
        return 0

    for d in near + far:
        cloud_copy(d).wait_recv()
        for s in range(1, sib):
            relay_copy(d, s).start()
    lax.fori_loop(1, memb, take_right, 0, unroll=7)
    for d in range(memb):
        for s in range(1, sib):
            relay_copy(d, s).wait_recv()
    lax.fori_loop(0, memb, take_relay, 0, unroll=4)
    def take_rows(turn):
        for d in turn:
            if d > 0:
                sup_copy(d).wait_recv()
        for d in turn:
            if d > 0:
                make_left(peer(d))
        for n, d in enumerate(turn):
            cost_rows(peer(d))
            if n > 0:
                raise_best(peer(turn[n - 1]))
        raise_best(peer(turn[-1]))

    take_rows([0] + near)
    take_rows(far)

    tiles = chunk // LANES
    groups = rows // GROUP
    unroll = groups if cols <= WIDE else 2

    def tile(g, base, c):
        return (
            pl.ds(pl.multiple_of(g * GROUP, GROUP), GROUP),
            pl.ds(pl.multiple_of(base + c * LANES, LANES), LANES),
        )

    def rows_of(ref, g):
        return ref[pl.ds(pl.multiple_of(g * GROUP, GROUP), GROUP), :]

    def fold(x, op):
        acc = x[0:8]
        for i in range(8, GROUP, 8):
            acc = op(acc, x[i:i + 8])
        return acc

    def lanes(ref, base, c):
        return ref[:, base + c * LANES:base + (c + 1) * LANES]

    high = jnp.max(best[...], axis=0, keepdims=True)
    stat_send[0] = high
    col[0] = jnp.broadcast_to(high, (8, cols))
    col[1] = jnp.broadcast_to(jnp.exp2(high), (8, cols))

    pieces = cols // chunk

    def high_copy(s):
        return pltpu.make_async_remote_copy(
            stat_send.at[0], stat_recv.at[s, 0],
            stat_ssem.at[0, s], stat_rsem.at[0, s],
            device_id=at(mine, lax.rem(r + s, sib)), device_id_type=pl.DeviceIdType.MESH)

    def stat_copy(step, n, s):
        span = pl.ds(n * chunk, chunk)
        place = 1 + step * pieces + n
        return pltpu.make_async_remote_copy(
            stat_send.at[1 + step, :, span], stat_recv.at[s, 1 + step, :, span],
            stat_ssem.at[place, s], stat_rsem.at[place, s],
            device_id=at(mine, lax.rem(r + s, sib)), device_id_type=pl.DeviceIdType.MESH)

    def take_stat(step, n):
        span = slice(n * chunk, n * chunk + chunk)
        for s in range(1, sib):
            if step == 0 and n == 0:
                high_copy(s).wait_recv()
            stat_copy(step, n, s).wait_recv()
        if step == 0:
            high = stat_send[0, :, span]
            for s in range(1, sib):
                high = jnp.maximum(high, stat_recv[s, 0, :, span])
            share[0, :, span] = jnp.exp2(stat_send[0, :, span] - high)
            for s in range(1, sib):
                share[s, :, span] = jnp.exp2(stat_recv[s, 0, :, span] - high)
        local = share[0, :, span]
        total = local * stat_send[1 + step, :, span]
        for s in range(1, sib):
            total = total + share[s, :, span] * stat_recv[s, 1 + step, :, span]
        col[1, :, span] = jnp.broadcast_to(local / (total * float(cols)), (8, chunk))

    for s in range(1, sib):
        high_copy(s).start()

    def times(x, y):
        return x * jnp.concatenate([y] * (GROUP // 8), axis=0)

    for step in range(ITERS):
        for base in range(0, cols, chunk):
            if step > 0:
                take_stat(step - 1, base // chunk)

            def row_step(g, _, base=base):
                acc = jnp.zeros((GROUP, LANES), F32)
                a = rows_of(top, g)
                for c in range(tiles):
                    k = mat[tile(g, base, c)]
                    if step == 0:
                        b = jnp.concatenate([lanes(col.at[0], base, c)] * (GROUP // 8), axis=0)
                        k = jnp.exp2((k - a) - b)
                        mat[tile(g, base, c)] = k
                    acc = acc + times(k, lanes(col.at[1], base, c))
                if base > 0:
                    acc = acc + rows_of(part, g)
                span = pl.ds(pl.multiple_of(g * GROUP, GROUP), GROUP)
                if base + chunk < cols:
                    part[span, :] = acc
                else:
                    total = jnp.sum(acc, axis=1, keepdims=True)
                    u_ref[span, :] = jnp.broadcast_to(1.0 / (total * rows_all(dims)), acc.shape)
                return 0

            lax.fori_loop(0, groups, row_step, 0, unroll=unroll)
        for base in range(0, cols, chunk):
            def col_step(g, acc, base=base):
                u = rows_of(u_ref, g)
                return tuple(
                    acc[c] + fold(mat[tile(g, base, c)] * u, jnp.add) for c in range(tiles))

            start = tuple(jnp.zeros((8, LANES), F32) for _ in range(tiles))
            acc = lax.fori_loop(0, groups, col_step, start, unroll=unroll)
            for c in range(tiles):
                stat_send[1 + step, :, base + c * LANES:base + (c + 1) * LANES] = jnp.sum(
                    acc[c], axis=0, keepdims=True)
            for s in range(1, sib):
                stat_copy(step, base // chunk, s).start()

    weight_sum = weights_ref[0]
    for k in range(1, memb):
        weight_sum = weight_sum + weights_ref[k]
    weight = weights_ref[mine] / weight_sum

    def out_copy(target):
        return pltpu.make_async_remote_copy(
            out_send.at[target], out_recv.at[mine], out_ssem.at[target], out_rsem.at[mine],
            device_id=at(target, r), device_id_type=pl.DeviceIdType.MESH)

    def out_arrival(source):
        return pltpu.make_async_remote_copy(
            out_send.at[source], out_recv.at[source], out_ssem.at[source], out_rsem.at[source],
            device_id=at(source, r), device_id_type=pl.DeviceIdType.MESH)

    def plan_columns(slot, block, base, width):
        u = u_ref[block * shard:(block + 1) * shard, :] * rows_all(dims)
        for j in range(0, width, LANES):
            span = pl.ds(base + j, LANES)
            p = mat[block * shard:(block + 1) * shard, span] * u
            v = jnp.concatenate([col[1, :, span]] * (shard // 8), axis=0)
            plan[slot, :, span] = (p * v).astype(BF16)

    for n in range(pieces):
        take_stat(ITERS - 1, n)
        plan_columns(0, ORDER[0], n * chunk, chunk)

    for turn in TURNS:
        for slot, block in enumerate(turn):
            if block != ORDER[0]:
                def plan_step(base, _):
                    plan_columns(slot, block, base, min(cols, WIDE))
                    return 0

                sweep(plan_step, 0)
            term = lax.dot_general(
                right[:dim, :], plan[slot], (((1,), (1,)), ((), ())), preferred_element_type=F32)
            out_send[block] = term * weight
        for block in turn:
            @pl.when(block != mine)
            def _():
                out_copy(block).start()

    total = out_send[mine]
    for d in range(1, memb):
        out_arrival(peer(d)).wait_recv()
        total = total + out_recv[peer(d)]
    out_ref[...] = total

    for d in range(1, memb):
        cloud_copy(d).wait_send()
        sup_copy(d).wait_send()
        out_copy(peer(d)).wait_send()
    for s in range(1, sib):
        for d in range(memb):
            relay_copy(d, s).wait_send()
        high_copy(s).wait_send()
        for step in range(ITERS):
            for n in range(pieces):
                stat_copy(step, n, s).wait_send()


def piece_of(cols):
    return cols // 2 if cols <= WIDE else WIDE


def rows_all(dims):
    memb, sib, shard, _ = dims
    return float(memb * sib * shard)


def per_device(support, clouds, member_weights):
    devices = lax.axis_size("pts")
    memb, shard, dim = clouds.shape
    sib = devices // memb
    rows, cols = memb * shard, devices * shard
    dims = (memb, sib, shard, dim)
    pieces = cols // piece_of(cols)
    vmem, dma = pltpu.VMEM, pltpu.SemaphoreType.DMA
    out = pl.pallas_call(
        functools.partial(kernel, dims),
        out_shape=jax.ShapeDtypeStruct((dim, shard), F32),
        in_specs=[
            pl.BlockSpec(memory_space=pltpu.HBM),
            pl.BlockSpec(memory_space=pltpu.HBM),
            pl.BlockSpec(memory_space=pltpu.HBM),
        ],
        out_specs=pl.BlockSpec(memory_space=pltpu.VMEM),
        scratch_shapes=[
            pltpu.SMEM((memb,), F32),
            vmem((memb, dim, shard), BF16),
            vmem((memb, dim, shard), BF16),
            vmem((devices, dim, shard), BF16),
            vmem((rows, 3 * dim + EXTRA), BF16),
            vmem((3 * dim + EXTRA, cols), BF16),
            vmem((rows, cols), F32),
            vmem((rows, LANES), F32),
            vmem((8, cols), F32),
            vmem((rows, LANES), F32),
            vmem((rows, LANES), F32),
            vmem((2, 8, cols), F32),
            vmem((sib, 1, cols), F32),
            vmem((1 + ITERS, 1, cols), F32),
            vmem((sib, 1 + ITERS, 1, cols), F32),
            vmem((3, shard, cols), BF16),
            vmem((memb, dim, shard), F32),
            vmem((memb, dim, shard), F32),
            dma((memb,)), dma((memb,)),
            dma((memb,)), dma((memb,)),
            dma((memb, sib)), dma((memb, sib)),
            dma((1 + ITERS * pieces, sib)), dma((1 + ITERS * pieces, sib)),
            dma((memb,)), dma((memb,)), dma((4,)),
        ],
        compiler_params=pltpu.CompilerParams(
            collective_id=0, has_side_effects=True,
            vmem_limit_bytes=rows * cols * 4 + (24 << 20)),
    )(*(pltpu.with_memory_space_constraint(x, pltpu.HBM)
        for x in (support.T, clouds.swapaxes(1, 2), member_weights)))
    return out.T


def solution(mesh):
    in_specs = (P(("grp", "pts"), None), P(None, ("grp", "pts"), None), P("grp"))
    out_specs = P(("grp", "pts"), None)
    return jax.shard_map(
        per_device, mesh=mesh, in_specs=in_specs, out_specs=out_specs, check_vma=False
    )
```
